256 devices in a mesh: loop: 2 (over core), group: 2 (over x_lo), rep: 64 (over z, y, x_hi).
Axes of the slice: x: 4 (x_hi: 2, x_lo: 2; x = x_hi * 2 + x_lo), y: 4, z: 8, core: 2. Of those that a mesh axis runs over, the one named last changes fastest.
Arguments:
- frames: bfloat16 [512, 256, 128], P(('loop', 'rep'), 'group'), may hold values from -6 to 6
- factors: bfloat16 [128, 256, 128], P(None, ('loop', 'group')), as said below
- comp_means: bfloat16 [256, 128], P(('loop', 'group')), may hold values from -3 to 3
- log_weights: bfloat16 [256], P(('loop', 'group')), may hold values from -4 to 4
- pair_lists: int32 [512, 2, 2, 4], P(('loop', 'rep'), 'group'), may hold values from 0 to 3, as said below
- counts: int32 [512, 2, 2], P(('loop', 'rep'), 'group'), may hold values from 1 to 4
Outputs:
- occupancy: float32 [256], P(('loop', 'group'))
- first_moment: float32 [256, 128], P(('loop', 'group'))
- second_moment: float32 [128, 256, 128], P(None, ('loop', 'group'))
- frame_loglik: float32 [512, 256], P(('loop', 'rep'), 'group')
The draws below stay inside these ranges and needn't reach their ends.
Inputs may be any that keep to these rules, and one draw needn't show every extreme that they name: Each pair_lists[b, g, l, :] is an ordering of the 4 blocks of that panel. `factors`: every factor is upper triangular with a positive diagonal.
All inputs are finite; a program needn't handle non-finite values.
Results may differ from the reference program's by a relative error of at most 0.002.
Values may be sent and summed in bfloat16 or wider, within the bound.
No kernel may reach another device: no remote copies, remote signals or barrier semaphores. Data moves between devices by JAX's collectives and lax.ppermute only.
A program may use at most 128 MiB of HBM per device.

```python
import math
import jax
import jax.numpy as jnp
from jax import lax

D = 128
KC = 64
CB = 16
PB = 4
FB = 256
NB = 512
K = 256
N_LOOP = 2
N_GROUP = 2


def draw_factors(key, part):
    first_key, second_key = jax.random.split(key)
    spread = jax.random.normal(first_key, (D, K, D), jnp.float32)
    upper_part = spread * (0.5 / math.sqrt(D))
    diagonal = jnp.exp(jax.random.uniform(second_key, (K, D), jnp.float32, math.log(0.8), math.log(1.25)))
    row_index = jnp.arange(D)[:, None, None]
    col_index = jnp.arange(D)[None, None, :]
    result = jnp.where(row_index == col_index, jnp.transpose(diagonal)[:, :, None], jnp.where(row_index < col_index, upper_part, 0.0))
    return result.astype(jnp.bfloat16)


def draw_pair_lists(key, part):
    scores = jax.random.randint(key, (NB, N_GROUP, N_LOOP, PB), 0, 1 << 20) * PB
    scores = scores + jnp.arange(PB, dtype=jnp.int32)
    return jnp.argsort(scores, axis=-1, stable=True).astype(jnp.int32)


def set_ends(values, key, least, high):
    place = [jax.random.randint(jax.random.fold_in(key, axis), (), 0, length) for axis, length in enumerate(values.shape)]
    widest = values.shape.index(max(values.shape))
    neighbour = place[:widest] + [(place[widest] + 1) % values.shape[widest]] + place[widest + 1:]
    return values.at[tuple(place)].set(least).at[tuple(neighbour)].set(high)


def block_scale(rng, dims, pieces, low, largest):
    def one(position, parts):
        heights = jax.random.uniform(jax.random.fold_in(jax.random.fold_in(rng, 6), position), (parts,), jnp.float32, low / len(pieces), largest / len(pieces))
        return jnp.repeat(jnp.exp(heights), dims[position] // parts).reshape((-1,) + (1,) * (len(dims) - position - 1))

    factor_of = one(*pieces[0])
    for cut in pieces[1:]:
        factor_of = factor_of * one(*cut)
    return factor_of


def noise(rng, extent, deviation, limit, pieces=(), kind=jnp.bfloat16):
    entries = jax.random.normal(rng, extent, jnp.float32) * deviation
    if len(pieces) > 0:
        entries = block_scale(rng, extent, pieces, -0.22, 0.18) * entries
    return jnp.clip(entries, min=-limit, max=limit).astype(kind)


def setup_inputs(seed: int = 0) -> dict:
    key_of = jax.random.split(jax.random.key(seed), 7)
    frames = noise(key_of[0], (NB, FB, D), 1.0, 6.0, ((0, 128), (1, 2)))
    factors = draw_factors(jax.random.fold_in(key_of[6], 71), 0)
    comp_means = noise(key_of[2], (K, D), 0.5, 3.0, ((0, 4),))
    log_weights = noise(key_of[3], (K,), 1.0, 4.0, ((0, 4),))
    pair_lists = draw_pair_lists(jax.random.fold_in(key_of[6], 71), 0)
    counts = set_ends(jax.random.randint(key_of[5], (NB, N_GROUP, N_LOOP), 1, PB + 1), jax.random.fold_in(key_of[5], 1), 1, PB).astype(jnp.int32)
    return {"frames": frames, "factors": factors, "comp_means": comp_means, "log_weights": log_weights, "pair_lists": pair_lists, "counts": counts}


half_log = 0.5 * math.log(2.0 * math.pi)


def reference(frames, factors, comp_means, log_weights, pair_lists, counts):
    blocks_all, block_rows, features = frames.shape
    panels = N_LOOP * N_GROUP
    frame_rows = frames.reshape(blocks_all * block_rows, features).astype(jnp.float32)
    dense = factors.astype(jnp.float32)
    centre = jnp.einsum('kd,dke->ke', comp_means.astype(jnp.float32), dense, precision=lax.Precision.HIGHEST)
    logdet = jnp.sum(jnp.log(jnp.einsum('iki->ki', dense)), axis=1)
    bias = log_weights.astype(jnp.float32) + logdet - half_log * features
    per_panel = jnp.moveaxis(dense.reshape(features, panels, KC * features), 1, 0)

    def panel_scores(inputs):
        flat, centre_part, bias_part = inputs
        product = jnp.dot(frame_rows, flat, precision=lax.Precision.HIGHEST)
        shifted = product.reshape(-1, KC, features) - centre_part
        return bias_part - 0.5 * jnp.sum(shifted * shifted, axis=-1)

    scores = lax.map(panel_scores, (per_panel, centre.reshape(panels, KC, features), bias.reshape(panels, KC)))
    slot_index = jnp.arange(PB, dtype=jnp.int32)
    in_use = slot_index < counts[..., None]
    hits = (pair_lists[..., None] == slot_index) & in_use[..., None]
    listed = jnp.any(hits, axis=3)
    ordered = jnp.transpose(listed, (2, 1, 0, 3)).reshape(panels, blocks_all, PB)
    allowed = jnp.repeat(ordered, CB, axis=2)[:, :, None, :]
    masked = jnp.where(allowed, scores.reshape(panels, blocks_all, block_rows, KC), -jnp.inf)
    highest = jnp.max(masked, axis=(0, 3))
    exp_total = jnp.sum(jnp.exp(masked - highest[None, :, :, None]), axis=(0, 3))
    loglik = highest + jnp.log(exp_total)
    weights = jnp.exp(masked - loglik[None, :, :, None]).astype(jnp.bfloat16)
    weights = weights.reshape(panels, blocks_all * block_rows, KC)

    def panel_stats(weights_part):
        wide = weights_part.astype(jnp.float32)
        rounded = lax.optimization_barrier((wide[:, :, None] * frame_rows[:, None, :]).astype(jnp.bfloat16))
        weighted = rounded.astype(jnp.float32)
        occupancy = jnp.sum(wide, axis=0)
        first_moment = jnp.sum(weighted, axis=0)
        second_moment = jnp.dot(frame_rows.T, weighted.reshape(-1, KC * features), precision=lax.Precision.HIGHEST)
        return occupancy, first_moment, second_moment

    occupancy, first_moment, second_moment = lax.map(panel_stats, weights)
    second_moment = second_moment.reshape(panels, features, KC, features)
    second_moment = jnp.transpose(second_moment, (1, 0, 2, 3)).reshape(features, panels * KC, features)
    return occupancy.reshape(-1), first_moment.reshape(-1, features), second_moment, loglik
```

```python
import functools
import math

import jax
import jax.numpy as jnp
from jax import lax
from jax.experimental import pallas as pl
from jax.experimental.pallas import tpu as pltpu
from jax.sharding import Mesh
from jax.sharding import PartitionSpec as P

D = 128
KC = 64
CB = 16
NF = 2048
SH = 512
ROWS = 72
HALF = 64

half_log = 0.5 * math.log(2.0 * math.pi)

Z_STEPS = (1, 2, 4)
BIT_VALUE = {3: 2 * Z_STEPS[0], 2: 2 * Z_STEPS[1], 1: 2 * Z_STEPS[2], 0: 1}


def spread_of(p):
    value = 0
    for bit, mask in BIT_VALUE.items():
        if p >> bit & 1:
            value ^= mask
    return value


SPREAD = [spread_of(p) for p in range(CB)]
PLACE = [SPREAD.index(v) for v in range(CB)]


def swap(value, axis, by):
    count = lax.axis_size(axis)
    return lax.ppermute(value, axis, [(i, i ^ by) for i in range(count)])


def swap_both(value):
    pairs = [(i, 3 - i) for i in range(4)]
    return lax.ppermute(value, ("loop", "group"), pairs)


def score_kernel(flags, x0, x1, x2, x3, at, means, log_weights, s_out, ms_out, xt_out, diag):
    step = pl.program_id(0)
    per = at.shape[0]

    @pl.when(step == 0)
    def _():
        for shard, ref in enumerate((x0, x1, x2, x3)):
            for part in range(SH // D):
                piece = ref[part * D : (part + 1) * D, :].astype(jnp.float32)
                start = shard * SH + part * D
                xt_out[:, start : start + D] = piece.T.astype(jnp.bfloat16)

    row = lax.broadcasted_iota(jnp.int32, (D, D), 0)
    col = lax.broadcasted_iota(jnp.int32, (D, D), 1)
    base = pl.multiple_of(step * per, per)
    mean_rows = means[pl.ds(base, per), :]
    centres = []
    diagonals = []
    for c in range(per):
        wide = at[c].astype(jnp.float32)
        centres.append(jnp.sum(wide * mean_rows[c : c + 1, :], axis=1, keepdims=True))
        diagonals.append(jnp.sum(jnp.where(row == col, wide, 0.0), axis=0, keepdims=True))
    diag[pl.ds(base, per), :] = jnp.concatenate(diagonals, axis=0)
    tile = 256
    for start in range(0, NF, tile):
        columns = xt_out[:, start : start + tile]
        sums = []
        for c in range(per):
            product = jnp.dot(at[c], columns, preferred_element_type=jnp.float32)
            shifted = product - centres[c]
            sums.append(jnp.sum(shifted * shifted, axis=0, keepdims=True))
        s_out[pl.ds(base, per), start : start + tile] = jnp.concatenate(sums, axis=0)

    @pl.when(step == pl.num_programs(0) - 1)
    def _():
        logdet = jnp.sum(jnp.log(diag[...]), axis=1, keepdims=True)
        bias = log_weights[...] + logdet - half_log * D
        for start in range(0, NF, D):
            shard, block = start // SH, (start % SH) // D
            pieces = []
            for q in range(KC // CB):
                allowed = flags[((shard // 2) * 4 + block) * 4 + q]
                part = s_out[q * CB : (q + 1) * CB, start : start + D]
                score = bias[q * CB : (q + 1) * CB, :] - 0.5 * part
                pieces.append(jnp.where(allowed > 0, score, -jnp.inf))
            masked = jnp.concatenate(pieces, axis=0)
            s_out[:, start : start + D] = masked
            highest = jnp.max(masked, axis=0, keepdims=True)
            ms_out[0:1, start : start + D] = highest
            ms_out[1:2, start : start + D] = jnp.sum(jnp.exp(masked - highest), axis=0, keepdims=True)


def scores_of(flags, shards, at, means, log_weights):
    per = 8
    whole = lambda shape: pl.BlockSpec(shape, lambda i, f: (0,) * len(shape))
    return pl.pallas_call(
        score_kernel,
        out_shape=(
            jax.ShapeDtypeStruct((KC, NF), jnp.float32),
            jax.ShapeDtypeStruct((2, NF), jnp.float32),
            jax.ShapeDtypeStruct((D, NF), jnp.bfloat16),
        ),
        grid_spec=pltpu.PrefetchScalarGridSpec(
            num_scalar_prefetch=1,
            grid=(KC // per,),
            in_specs=[whole((SH, D))] * 4
            + [pl.BlockSpec((per, D, D), lambda i, f: (i, 0, 0)), whole((KC, D)), whole((KC, 1))],
            out_specs=[whole((KC, NF)), whole((2, NF)), whole((D, NF))],
            scratch_shapes=[pltpu.VMEM((KC, D), jnp.float32)],
        ),
        cost_estimate=pl.CostEstimate(
            flops=2 * KC * D * D * NF, bytes_accessed=4 << 20, transcendentals=KC * NF
        ),
        name="scores",
    )(flags, *shards, at, means, log_weights)


def log_total(parts, shard):
    rows = []
    for d, ref in enumerate(parts):
        start = (shard ^ d) * SH
        rows.append((ref[0:1, start : start + SH], ref[1:2, start : start + SH]))
    highest = functools.reduce(jnp.maximum, [m for m, _ in rows])
    total = sum(s * jnp.exp(m - highest) for m, s in rows)
    return highest + jnp.log(total)


def split_pair(value):
    high = value.astype(jnp.bfloat16).astype(jnp.float32)
    return high, value - high


def moment_kernel(own, meta, x0, x1, x2, x3, xt, scores, m0, m1, m2, m3, *refs):
    outs, (weights, left) = refs[:-2], refs[-2:]
    packed = outs[0]
    parts = (m0, m1, m2, m3)
    xs = (x0, x1, x2, x3)
    first = jnp.zeros((CB, D), jnp.float32)
    occupancy = jnp.zeros((CB, 1), jnp.float32)
    for shard in range(4):
        span = slice(shard * SH, (shard + 1) * SH)
        loglik = log_total(parts, shard)
        if own and shard == 0:
            outs[1][...] = loglik
        part = jnp.exp(scores[:, span] - loglik).astype(jnp.bfloat16)
        wide = part.astype(jnp.float32)
        weights[:, span] = wide
        occupancy += jnp.sum(wide, axis=1, keepdims=True)
        first += jnp.dot(part, xs[shard][...], preferred_element_type=jnp.float32)
    left_rows = left.shape[1]
    per = left_rows // D
    first_ref, occupancy_ref = outs[-2], outs[-1]
    first_ref[...] = first
    occupancy_ref[...] = jnp.broadcast_to(occupancy, (CB, D))
    row = lax.broadcasted_iota(jnp.int32, (D, D), 0)
    col = lax.broadcasted_iota(jnp.int32, (D, D), 1)
    row_half = lax.broadcasted_iota(jnp.int32, (HALF, D), 0)
    col_half = lax.broadcasted_iota(jnp.int32, (HALF, D), 1)
    keep_top = (col_half >= HALF) | (col_half >= row_half)
    for group in range(CB // per):
        buffer = left.at[group % left.shape[0]]
        places = []
        for c in range(per):
            p = group * per + c
            place = meta[1] ^ SPREAD[p]
            places.append(place)
            line = weights[pl.ds(place, 1), :].astype(jnp.bfloat16)
            buffer[c * D : (c + 1) * D, :] = xt[...] * line
        gram = None
        for shard in range(4):
            term = jnp.dot(
                buffer[:, shard * SH : (shard + 1) * SH],
                xs[shard][...],
                preferred_element_type=jnp.float32,
            )
            gram = term if gram is None else gram + term
        for c in range(per):
            p = group * per + c
            one = gram[c * D : (c + 1) * D, :]
            diagonal = jnp.sum(jnp.where(row == col, one, 0.0), axis=0, keepdims=True)
            moved = pltpu.roll(one[HALF:, :], HALF, 1)
            triangle = jnp.where(keep_top, one[:HALF, :], moved)
            extras = [
                occupancy_ref[pl.ds(places[c], 1), :],
                first_ref[pl.ds(places[c], 1), :],
                diagonal,
            ]
            zero = jnp.zeros((1, D), jnp.float32)
            if own:
                tail = extras + [zero] * 5
            else:
                pairs = [split_pair(v) for v in extras]
                tail = [h for h, _ in pairs] + [l for _, l in pairs] + [zero] * 2
            packed[p, 0:HALF, :] = triangle.astype(packed.dtype)
            packed[p, HALF:ROWS, :] = jnp.concatenate(tail, axis=0).astype(packed.dtype)


def moments_of(chunk, meta, shards, xt, scores, partials):
    own = chunk == 0
    whole = lambda shape: pl.BlockSpec(shape, lambda i, f: (0,) * len(shape))
    out_shape = [jax.ShapeDtypeStruct((CB, ROWS, D), jnp.float32 if own else jnp.bfloat16)]
    out_specs = [whole((CB, ROWS, D))]
    if own:
        out_shape.append(jax.ShapeDtypeStruct((1, SH), jnp.float32))
        out_specs.append(whole((1, SH)))
    result = pl.pallas_call(
        functools.partial(moment_kernel, own),
        out_shape=tuple(out_shape),
        grid_spec=pltpu.PrefetchScalarGridSpec(
            num_scalar_prefetch=1,
            grid=(1,),
            in_specs=[whole((SH, D))] * 4
            + [whole((D, NF)), pl.BlockSpec((CB, NF), lambda i, f: (f[0] ^ chunk, 0))]
            + [whole((2, NF))] * 4,
            out_specs=out_specs,
            scratch_shapes=[
                pltpu.VMEM((CB, D), jnp.float32),
                pltpu.VMEM((CB, D), jnp.float32),
                pltpu.VMEM((CB, NF), jnp.float32),
                pltpu.VMEM((2, 4 * D, NF), jnp.bfloat16),
            ],
        ),
        cost_estimate=pl.CostEstimate(
            flops=2 * CB * D * D * NF, bytes_accessed=2 << 20, transcendentals=CB * NF
        ),
        name="moments_own" if own else "moments",
    )(meta, *shards, xt, scores, *partials)
    return result if own else result[0]


def unpack_kernel(chunk, meta, packed, *refs):
    second, first, occupancy = refs[-3:]
    group = pl.program_id(0)
    row = lax.broadcasted_iota(jnp.int32, (D, D), 0)
    col = lax.broadcasted_iota(jnp.int32, (D, D), 1)
    unit = (row == col).astype(jnp.bfloat16)
    row_half = lax.broadcasted_iota(jnp.int32, (HALF, D), 0)
    col_half = lax.broadcasted_iota(jnp.int32, (HALF, D), 1)
    upper = (col_half >= HALF) | (col_half >= row_half)
    lower = (col_half < HALF) | (col_half - HALF < row_half)
    for c in range(8):
        p = meta[2 + group * 8 + c]
        tile = packed[p, 0:HALF, :]
        extra = packed[p, HALF:ROWS, :].astype(jnp.float32)
        occupancy[c : c + 1, :] = extra[0:1, :] + extra[3:4, :]
        first[c : c + 1, :] = extra[1:2, :] + extra[4:5, :]
        diagonal = extra[2:3, :] + extra[5:6, :]
        turned = lax.dot_general(
            unit, tile, (((1,), (1,)), ((), ())), preferred_element_type=jnp.float32
        )
        wide = tile.astype(jnp.float32)
        both = jnp.concatenate([turned[:HALF, :], wide[:, :HALF]], axis=1)
        top = jnp.where(upper, wide, both)
        other = jnp.concatenate([turned[HALF:, :], wide[:, :HALF]], axis=1)
        mirror = jnp.concatenate([turned[HALF:, :], turned[:HALF, :]], axis=1)
        bottom = jnp.where(lower, other, mirror)
        full = jnp.concatenate([top, bottom], axis=0)
        second[:, c, :] = jnp.where(row == col, diagonal, full)


def unpack(chunk, meta, packed, earlier):
    whole = lambda shape: pl.BlockSpec(shape, lambda i, f: (0,) * len(shape))
    place = lambda i, f: (f[0] ^ chunk) * 2 + i
    return pl.pallas_call(
        functools.partial(unpack_kernel, chunk),
        out_shape=(
            jax.ShapeDtypeStruct((D, KC, D), jnp.float32),
            jax.ShapeDtypeStruct((KC, D), jnp.float32),
            jax.ShapeDtypeStruct((KC, D), jnp.float32),
        ),
        grid_spec=pltpu.PrefetchScalarGridSpec(
            num_scalar_prefetch=1,
            grid=(2,),
            in_specs=[whole((CB, ROWS, D))]
            + [pl.BlockSpec(memory_space=pl.ANY)] * len(earlier),
            out_specs=[
                pl.BlockSpec((D, 8, D), lambda i, f: (0, place(i, f), 0)),
                pl.BlockSpec((8, D), lambda i, f: (place(i, f), 0)),
                pl.BlockSpec((8, D), lambda i, f: (place(i, f), 0)),
            ],
        ),
        input_output_aliases={2 + n: n for n in range(len(earlier))},
        cost_estimate=pl.CostEstimate(
            flops=2 * CB * D * D * HALF, bytes_accessed=2 << 20, transcendentals=0
        ),
        name="unpack",
    )(meta, packed, *earlier)


def per_device(frames, factors, comp_means, log_weights, pair_lists, counts):
    own = frames.reshape(SH, D)
    shards = (own, swap(own, "group", 1), swap(own, "loop", 1), swap_both(own))

    loop_index = lax.axis_index("loop")
    y_index, z_index, x_index = (lax.axis_index(a) for a in ("y", "z", "xh"))
    low = z_index * 2 + x_index

    slots = jnp.arange(4, dtype=jnp.int32)
    in_use = slots < counts[:, 0, :, None]
    hits = (pair_lists[:, 0, :, :, None] == slots) & in_use[..., None]
    listed = jnp.any(hits, axis=2).astype(jnp.int32)
    mine = lax.dynamic_index_in_dim(listed, loop_index, 1, keepdims=False)
    theirs = lax.dynamic_index_in_dim(listed, 1 - loop_index, 1, keepdims=False)
    flags = jnp.concatenate([mine.reshape(-1), swap(theirs, "loop", 1).reshape(-1)])

    spots = jnp.arange(CB, dtype=jnp.int32) ^ low
    place = jnp.zeros_like(spots)
    for bit in range(4):
        place = place ^ (((spots >> bit) & 1) * PLACE[1 << bit])
    meta = jnp.concatenate([jnp.stack([y_index, low]).astype(jnp.int32), place])

    at = jnp.transpose(factors, (1, 2, 0))
    scores, partial, xt = scores_of(
        flags, shards, at, comp_means.astype(jnp.float32), log_weights.astype(jnp.float32)[:, None]
    )
    partials = (partial, swap(partial, "group", 1), swap(partial, "loop", 1), swap_both(partial))

    arrived = []
    for chunk in (1, 2, 3):
        packed = moments_of(chunk, meta, shards, xt, scores, partials)
        arrived.append(swap(packed, "y", chunk))
    total, loglik = moments_of(0, meta, shards, xt, scores, partials)
    for piece in arrived:
        total = total + piece.astype(jnp.float32)

    for step in Z_STEPS:
        half = total.shape[0] // 2
        total = total[:half] + swap(total[half:], "z", step)
    total = total[:1] + swap(total[1:], "xh", 1)

    extras = total[:, HALF : HALF + 3] + total[:, HALF + 3 : HALF + 6]
    high = extras.astype(jnp.bfloat16)
    rest = (extras - high.astype(jnp.float32)).astype(jnp.bfloat16)
    spare = jnp.zeros((1, 2, D), jnp.bfloat16)
    held = jnp.concatenate([total[:, :HALF].astype(jnp.bfloat16), high, rest, spare], axis=1)
    held = jnp.concatenate([held, swap(held, "xh", 1)], axis=0)
    for step in reversed(Z_STEPS):
        held = jnp.concatenate([held, swap(held, "z", step)], axis=0)

    pieces = [held] + [swap(held, "y", chunk) for chunk in (1, 2, 3)]
    outs = ()
    for chunk, piece in enumerate(pieces):
        outs = unpack(chunk, meta, piece, outs)
    second, first, occupancy = outs
    return occupancy[:, 0], first, second, loglik.reshape(4, D)


def solution(mesh):
    rep = mesh.shape["rep"]
    fine = Mesh(
        mesh.devices.reshape(2, 2, rep // 8, 4, 2), ("loop", "group", "z", "y", "xh")
    )
    reps = ("z", "y", "xh")
    return jax.shard_map(
        per_device,
        mesh=fine,
        in_specs=(
            P(("loop",) + reps, "group", None),
            P(None, ("loop", "group"), None),
            P(("loop", "group"), None),
            P(("loop", "group")),
            P(("loop",) + reps, "group", None, None),
            P(("loop",) + reps, "group", None),
        ),
        out_specs=(
            P(("loop", "group")),
            P(("loop", "group"), None),
            P(None, ("loop", "group"), None),
            P(("loop",) + reps, "group"),
        ),
        check_vma=False,
    )
```

```python
import functools
import math

import jax
import jax.numpy as jnp
from jax import lax
from jax.experimental import pallas as pl
from jax.experimental.pallas import tpu as pltpu
from jax.sharding import Mesh
from jax.sharding import PartitionSpec as P

D = 128
KC = 64
CB = 16
NF = 2048
SH = 512
PER = 4
ROWS = 72
HALF = 64

LIMIT = pltpu.CompilerParams(vmem_limit_bytes=24 << 20)

SPAN = 240.0

half_log = 0.5 * math.log(2.0 * math.pi)

Z_STEPS = (1, 2, 7)


def swap(value, axis, by):
    count = lax.axis_size(axis)
    return lax.ppermute(value, axis, [(i, i ^ by) for i in range(count)])


def swap_both(value):
    pairs = [(i, 3 - i) for i in range(4)]
    return lax.ppermute(value, ("loop", "group"), pairs)


def score_kernel(flags, x0, x1, x2, x3, at, means, log_weights, s_out, ms_out, xt_out, diag):
    step = pl.program_id(0)
    per = at.shape[0]

    @pl.when(step == 0)
    def _():
        for shard, ref in enumerate((x0, x1, x2, x3)):
            for part in range(SH // D):
                piece = ref[part * D : (part + 1) * D, :].astype(jnp.float32)
                start = shard * SH + part * D
                xt_out[:, start : start + D] = piece.T.astype(jnp.bfloat16)

    row = lax.broadcasted_iota(jnp.int32, (D, D), 0)
    col = lax.broadcasted_iota(jnp.int32, (D, D), 1)
    base = pl.multiple_of(step * per, per)
    mean_rows = means[pl.ds(base, per), :].astype(jnp.float32)
    centres = []
    diagonals = []
    for c in range(per):
        wide = at[c].astype(jnp.float32)
        centres.append(jnp.sum(wide * mean_rows[c : c + 1, :], axis=1, keepdims=True))
        diagonals.append(jnp.sum(jnp.where(row == col, wide, 0.0), axis=0, keepdims=True))
    diag[pl.ds(base, per), :] = jnp.concatenate(diagonals, axis=0)
    tile = 256
    for start in range(0, NF, tile):
        columns = xt_out[:, start : start + tile]
        sums = []
        stacked = at[...].reshape(per * D, D)
        products = jnp.dot(stacked, columns, preferred_element_type=jnp.float32)
        for c in range(per):
            shifted = products[c * D : (c + 1) * D, :] - centres[c]
            sums.append(jnp.sum(shifted * shifted, axis=0, keepdims=True))
        s_out[pl.ds(base, per), start : start + tile] = jnp.concatenate(sums, axis=0)

    @pl.when(step == pl.num_programs(0) - 1)
    def _():
        logdet = jnp.sum(jnp.log(diag[...]), axis=1, keepdims=True)
        bias = log_weights[...] + logdet - half_log * D
        for start in range(0, NF, D):
            shard, block = start // SH, (start % SH) // D
            pieces = []
            for q in range(KC // CB):
                allowed = flags[((shard // 2) * 4 + block) * 4 + q]
                part = s_out[q * CB : (q + 1) * CB, start : start + D]
                score = bias[q * CB : (q + 1) * CB, :] - 0.5 * part
                pieces.append(jnp.where(allowed > 0, score, -jnp.inf))
            masked = jnp.concatenate(pieces, axis=0)
            s_out[:, start : start + D] = masked
            highest = jnp.max(masked, axis=0, keepdims=True)
            ms_out[0:1, start : start + D] = highest
            ms_out[1:2, start : start + D] = jnp.sum(jnp.exp(masked - highest), axis=0, keepdims=True)


def scores_of(flags, shards, at, means, log_weights):
    per = 8
    whole = lambda shape: pl.BlockSpec(shape, lambda i, f: (0,) * len(shape))
    return pl.pallas_call(
        score_kernel,
        out_shape=(
            jax.ShapeDtypeStruct((KC, NF), jnp.float32),
            jax.ShapeDtypeStruct((2, NF), jnp.float32),
            jax.ShapeDtypeStruct((D, NF), jnp.bfloat16),
        ),
        grid_spec=pltpu.PrefetchScalarGridSpec(
            num_scalar_prefetch=1,
            grid=(KC // per,),
            in_specs=[whole((SH, D))] * 4
            + [pl.BlockSpec((per, D, D), lambda i, f: (i, 0, 0)), whole((KC, D)), whole((KC, 1))],
            out_specs=[whole((KC, NF)), whole((2, NF)), whole((D, NF))],
            scratch_shapes=[pltpu.VMEM((KC, D), jnp.float32)],
        ),
        cost_estimate=pl.CostEstimate(
            flops=2 * KC * D * D * NF, bytes_accessed=4 << 20, transcendentals=KC * NF
        ),
        compiler_params=LIMIT,
        name="scores",
    )(flags, *shards, at, means, log_weights)


def log_total(parts, shard):
    rows = []
    for d, ref in enumerate(parts):
        start = (shard ^ d) * SH
        rows.append((ref[0:1, start : start + SH], ref[1:2, start : start + SH]))
    highest = functools.reduce(jnp.maximum, [m for m, _ in rows])
    total = sum(s * jnp.exp(m - highest) for m, s in rows)
    return highest + jnp.log(total)


def split_pair(value):
    high = value.astype(jnp.bfloat16).astype(jnp.float32)
    return high, value - high


def moment_kernel(own, meta, x0, x1, x2, x3, xt, scores, m0, m1, m2, m3, *refs):
    outs, (weights, left) = refs[:-2], refs[-2:]
    packed = outs[0]
    parts = (m0, m1, m2, m3)
    xs = (x0, x1, x2, x3)
    first = jnp.zeros((CB, D), jnp.float32)
    occupancy = jnp.zeros((CB, 1), jnp.float32)
    for shard in range(4):
        span = slice(shard * SH, (shard + 1) * SH)
        loglik = log_total(parts, shard)
        if own and shard == 0:
            outs[1][...] = loglik
        part = jnp.exp(scores[:, span] - loglik).astype(jnp.bfloat16)
        wide = part.astype(jnp.float32)
        weights[:, span] = wide
        occupancy += jnp.sum(wide, axis=1, keepdims=True)
        first += jnp.dot(part, xs[shard][...], preferred_element_type=jnp.float32)
    left_rows = left.shape[1]
    per = left_rows // D
    first_ref, occupancy_ref = outs[-2], outs[-1]
    first_ref[...] = first
    occupancy_ref[...] = jnp.broadcast_to(occupancy, (CB, D))
    row = lax.broadcasted_iota(jnp.int32, (D, D), 0)
    col = lax.broadcasted_iota(jnp.int32, (D, D), 1)
    row_half = lax.broadcasted_iota(jnp.int32, (HALF, D), 0)
    col_half = lax.broadcasted_iota(jnp.int32, (HALF, D), 1)
    keep_top = (col_half >= HALF) | (col_half >= row_half)
    for group in range(CB // per):
        places = [meta[1] ^ (group * per + c) for c in range(per)]
        buffer = left.at[group % left.shape[0]]
        for c in range(per):
            line = weights[pl.ds(places[c], 1), :].astype(jnp.bfloat16)
            buffer[c * D : (c + 1) * D, :] = xt[...] * line
        gram = None
        for shard in range(4):
            part = buffer[:, shard * SH : (shard + 1) * SH]
            term = jnp.dot(part, xs[shard][...], preferred_element_type=jnp.float32)
            gram = term if gram is None else gram + term
        for c in range(per):
            p = group * per + c
            one = gram[c * D : (c + 1) * D, :]
            diagonal = jnp.sum(jnp.where(row == col, one, 0.0), axis=0, keepdims=True)
            moved = pltpu.roll(one[HALF:, :], HALF, 1)
            triangle = jnp.where(keep_top, one[:HALF, :], moved)
            extras = [
                occupancy_ref[pl.ds(places[c], 1), :],
                first_ref[pl.ds(places[c], 1), :],
                diagonal,
            ]
            zero = jnp.zeros((1, D), jnp.float32)
            if own:
                tail = extras + [zero] * 5
            else:
                pairs = [split_pair(v) for v in extras]
                tail = [h for h, _ in pairs] + [l for _, l in pairs] + [zero] * 2
            packed[p, 0:HALF, :] = triangle.astype(packed.dtype)
            packed[p, HALF:ROWS, :] = jnp.concatenate(tail, axis=0).astype(packed.dtype)


def moments_of(chunk, meta, shards, xt, scores, partials):
    own = chunk == 0
    whole = lambda shape: pl.BlockSpec(shape, lambda i, f: (0,) * len(shape))
    out_shape = [jax.ShapeDtypeStruct((CB, ROWS, D), jnp.float32 if own else jnp.bfloat16)]
    out_specs = [whole((CB, ROWS, D))]
    if own:
        out_shape.append(jax.ShapeDtypeStruct((1, SH), jnp.float32))
        out_specs.append(whole((1, SH)))
    result = pl.pallas_call(
        functools.partial(moment_kernel, own),
        out_shape=tuple(out_shape),
        grid_spec=pltpu.PrefetchScalarGridSpec(
            num_scalar_prefetch=1,
            grid=(1,),
            in_specs=[whole((SH, D))] * 4
            + [whole((D, NF)), pl.BlockSpec((CB, NF), lambda i, f: (f[0] ^ chunk, 0))]
            + [whole((2, NF))] * 4,
            out_specs=out_specs,
            scratch_shapes=[
                pltpu.VMEM((CB, D), jnp.float32),
                pltpu.VMEM((CB, D), jnp.float32),
                pltpu.VMEM((CB, NF), jnp.float32),
                pltpu.VMEM((2, PER * D, NF), jnp.bfloat16),
            ],
        ),
        cost_estimate=pl.CostEstimate(
            flops=2 * CB * D * D * NF, bytes_accessed=2 << 20, transcendentals=CB * NF
        ),
        compiler_params=LIMIT,
        name="moments_own" if own else "moments",
    )(meta, *shards, xt, scores, *partials)
    return result if own else result[0]


def unpack_kernel(chunk, meta, packed, *refs):
    second, first, occupancy = refs[-3:]
    group = pl.program_id(0)
    lane = lax.broadcasted_iota(jnp.int32, (1, D), 1)

    @pl.when(group == 0)
    def _():
        occupancy[...] = refs[2][...] if chunk else jnp.zeros((1, D), jnp.float32)

    occupied = occupancy[...]
    row = lax.broadcasted_iota(jnp.int32, (D, D), 0)
    col = lax.broadcasted_iota(jnp.int32, (D, D), 1)
    unit = (row == col).astype(jnp.bfloat16)
    row_half = lax.broadcasted_iota(jnp.int32, (HALF, D), 0)
    col_half = lax.broadcasted_iota(jnp.int32, (HALF, D), 1)
    upper = (col_half >= HALF) | (col_half >= row_half)
    lower = (col_half < HALF) | (col_half - HALF < row_half)
    for c in range(8):
        p = meta[1] ^ (group * 8 + c)
        tile = packed[p, 0:HALF, :]
        extra = packed[p, HALF:ROWS, :].astype(jnp.float32)
        here = (meta[0] ^ chunk) * CB + group * 8 + c
        occupied = jnp.where(lane == here, extra[0:1, :] + extra[3:4, :], occupied)
        first[c : c + 1, :] = extra[1:2, :] + extra[4:5, :]
        diagonal = extra[2:3, :] + extra[5:6, :]
        largest = jnp.max(diagonal, axis=1, keepdims=True) * (1.0 / SPAN)
        turned = lax.dot_general(
            unit, tile, (((1,), (1,)), ((), ())), preferred_element_type=jnp.float32
        )
        wide = tile.astype(jnp.float32)
        both = jnp.concatenate([turned[:HALF, :], wide[:, :HALF]], axis=1)
        top = jnp.where(upper, wide, both)
        other = jnp.concatenate([turned[HALF:, :], wide[:, :HALF]], axis=1)
        mirror = jnp.concatenate([turned[HALF:, :], turned[:HALF, :]], axis=1)
        bottom = jnp.where(lower, other, mirror)
        full = jnp.concatenate([top, bottom], axis=0)
        size = (jnp.log2(jnp.abs(full)) + SPAN / 2) * largest
        entry = jnp.where(full < 0, -size, size)
        second[:, c, :] = jnp.where(row == col, diagonal, entry)
    occupancy[...] = occupied


def unpack(chunk, meta, packed, earlier):
    whole = lambda shape: pl.BlockSpec(shape, lambda i, f: (0,) * len(shape))
    place = lambda i, f: (f[0] ^ chunk) * 2 + i
    return pl.pallas_call(
        functools.partial(unpack_kernel, chunk),
        out_shape=(
            jax.ShapeDtypeStruct((D, KC, D), jnp.float32),
            jax.ShapeDtypeStruct((KC, D), jnp.float32),
            jax.ShapeDtypeStruct((1, D), jnp.float32),
        ),
        grid_spec=pltpu.PrefetchScalarGridSpec(
            num_scalar_prefetch=1,
            grid=(2,),
            in_specs=[whole((CB, ROWS, D))]
            + [pl.BlockSpec(memory_space=pl.ANY)] * len(earlier[:2])
            + [whole((1, D))] * len(earlier[2:]),
            out_specs=[
                pl.BlockSpec((D, 8, D), lambda i, f: (0, place(i, f), 0)),
                pl.BlockSpec((8, D), lambda i, f: (place(i, f), 0)),
                whole((1, D)),
            ],
        ),
        input_output_aliases={2 + n: n for n in range(len(earlier[:2]))},
        cost_estimate=pl.CostEstimate(
            flops=2 * CB * D * D * HALF, bytes_accessed=2 << 20, transcendentals=0
        ),
        compiler_params=LIMIT,
        name="unpack",
    )(meta, packed, *earlier)


def packed_pairs(total, coded):
    extras = total[:, HALF : HALF + 3] + total[:, HALF + 3 : HALF + 6]
    high = lax.reduce_precision(extras, 8, 7)
    rest = (extras - high).astype(jnp.bfloat16)
    high = high.astype(jnp.bfloat16)
    spare = jnp.zeros((total.shape[0], 2, D), jnp.bfloat16)
    entries = total[:, :HALF]
    if coded:
        largest = jnp.max(extras[:, 2:3], axis=2, keepdims=True)
        size = jnp.minimum(jnp.abs(entries) / jnp.maximum(largest, 1e-30), 1.02)
        code = jnp.exp2(SPAN * size - SPAN / 2)
        entries = jnp.where(entries < 0, -code, code)
    return jnp.concatenate([entries.astype(jnp.bfloat16), high, rest, spare], axis=1)


def per_device(frames, factors, comp_means, log_weights, pair_lists, counts):
    own = frames.reshape(SH, D)
    shards = (own, swap(own, "group", 1), swap(own, "loop", 1), swap_both(own))

    loop_index = lax.axis_index("loop")
    z_index = lax.axis_index("z")
    top = z_index >> 2
    low = (((z_index & 1) ^ top) * 8) + ((((z_index >> 1) & 1) ^ top) * 4)

    slots = jnp.arange(4, dtype=jnp.int32)
    in_use = slots < counts[:, 0, :, None]
    hits = (pair_lists[:, 0, :, :, None] == slots) & in_use[..., None]
    listed = jnp.any(hits, axis=2).astype(jnp.int32)
    mine = lax.dynamic_index_in_dim(listed, loop_index, 1, keepdims=False)
    theirs = lax.dynamic_index_in_dim(listed, 1 - loop_index, 1, keepdims=False)
    flags = jnp.concatenate([mine.reshape(-1), swap(theirs, "loop", 1).reshape(-1)])

    meta = jnp.stack([lax.axis_index("y"), low]).astype(jnp.int32)

    at = jnp.transpose(factors, (1, 2, 0))
    scores, partial, xt = scores_of(
        flags, shards, at, comp_means, log_weights.astype(jnp.float32)[:, None]
    )
    partials = (partial, swap(partial, "group", 1), swap(partial, "loop", 1), swap_both(partial))

    arrived = []
    for chunk in (1, 2, 3):
        packed = moments_of(chunk, meta, shards, xt, scores, partials)
        arrived.append(swap(packed, "y", chunk))
    total, loglik = moments_of(0, meta, shards, xt, scores, partials)
    for piece in arrived:
        total = total + piece.astype(jnp.float32)

    for step in Z_STEPS[:2]:
        half = total.shape[0] // 2
        total = total[:half] + swap(packed_pairs(total[half:], False), "z", step)
    total = total + swap(total, "z", Z_STEPS[2])
    total = total + swap(total, "xh", 1)

    held = packed_pairs(total, True)
    for step in reversed(Z_STEPS[:2]):
        held = jnp.concatenate([held, swap(held, "z", step)], axis=0)

    pieces = [held] + [swap(held, "y", chunk) for chunk in (1, 2, 3)]
    outs = ()
    for chunk, piece in enumerate(pieces):
        outs = unpack(chunk, meta, piece, outs)
    second, first, occupancy = outs
    return occupancy[0, :KC], first, second, loglik.reshape(4, D)


def solution(mesh):
    rep = mesh.shape["rep"]
    fine = Mesh(
        mesh.devices.reshape(2, 2, rep // 8, 4, 2), ("loop", "group", "z", "y", "xh")
    )
    reps = ("z", "y", "xh")
    return jax.shard_map(
        per_device,
        mesh=fine,
        in_specs=(
            P(("loop",) + reps, "group", None),
            P(None, ("loop", "group"), None),
            P(("loop", "group"), None),
            P(("loop", "group")),
            P(("loop",) + reps, "group", None, None),
            P(("loop",) + reps, "group", None),
        ),
        out_specs=(
            P(("loop", "group")),
            P(("loop", "group"), None),
            P(None, ("loop", "group"), None),
            P(("loop",) + reps, "group"),
        ),
        check_vma=False,
    )
```

```python
import functools
import math

import jax
import jax.numpy as jnp
from jax import lax
from jax.experimental import pallas as pl
from jax.experimental.pallas import tpu as pltpu
from jax.sharding import Mesh
from jax.sharding import PartitionSpec as P

D = 128
KC = 64
CB = 16
NF = 2048
SH = 512
PER = 4
ROWS = 72
HALF = 64

LIMIT = pltpu.CompilerParams(vmem_limit_bytes=24 << 20)

SPAN = 240.0

half_log = 0.5 * math.log(2.0 * math.pi)

Z_STEPS = (1, 2, 7)


def swap(value, axis, by):
    count = lax.axis_size(axis)
    return lax.ppermute(value, axis, [(i, i ^ by) for i in range(count)])


def swap_both(value):
    pairs = [(i, 3 - i) for i in range(4)]
    return lax.ppermute(value, ("loop", "group"), pairs)


def score_kernel(panel, list0, list1, size0, size1, x0, x1, x2, x3, at, means, log_weights, s_out, ms_out, xt_out, diag):
    step = pl.program_id(0)
    per = at.shape[0]

    @pl.when(step == 0)
    def _():
        for shard, ref in enumerate((x0, x1, x2, x3)):
            for part in range(SH // D):
                piece = ref[part * D : (part + 1) * D, :].astype(jnp.float32)
                start = shard * SH + part * D
                xt_out[:, start : start + D] = piece.T.astype(jnp.bfloat16)

    row = lax.broadcasted_iota(jnp.int32, (D, D), 0)
    col = lax.broadcasted_iota(jnp.int32, (D, D), 1)
    base = pl.multiple_of(step * per, per)
    mean_rows = means[pl.ds(base, per), :].astype(jnp.float32)
    centres = []
    diagonals = []
    for c in range(per):
        wide = at[c].astype(jnp.float32)
        centres.append(jnp.sum(wide * mean_rows[c : c + 1, :], axis=1, keepdims=True))
        diagonals.append(jnp.sum(jnp.where(row == col, wide, 0.0), axis=0, keepdims=True))
    diag[pl.ds(base, per), :] = jnp.concatenate(diagonals, axis=0)
    tile = 256
    for start in range(0, NF, tile):
        columns = xt_out[:, start : start + tile]
        sums = []
        stacked = at[...].reshape(per * D, D)
        products = jnp.dot(stacked, columns, preferred_element_type=jnp.float32)
        for c in range(per):
            shifted = products[c * D : (c + 1) * D, :] - centres[c]
            sums.append(jnp.sum(shifted * shifted, axis=0, keepdims=True))
        s_out[pl.ds(base, per), start : start + tile] = jnp.concatenate(sums, axis=0)

    @pl.when(step == pl.num_programs(0) - 1)
    def _():
        logdet = jnp.sum(jnp.log(diag[...]), axis=1, keepdims=True)
        row_k = lax.broadcasted_iota(jnp.int32, (KC, KC), 0)
        col_k = lax.broadcasted_iota(jnp.int32, (KC, KC), 1)
        spread = jnp.where(row_k == col_k, log_weights[...].astype(jnp.float32), 0.0)
        bias = jnp.sum(spread, axis=1, keepdims=True) + logdet - half_log * D
        listed = []
        for lists, sizes in ((list0, size0), (list1, size1)):
            for block in range(4):
                bits = 0
                for slot in range(KC // CB):
                    bit = jnp.left_shift(1, lists[block, 0, panel[0], slot])
                    bits = bits | jnp.where(slot < sizes[block, 0, panel[0]], bit, 0)
                listed.append(bits)
        for start in range(0, NF, D):
            shard, block = start // SH, (start % SH) // D
            pieces = []
            for q in range(KC // CB):
                allowed = listed[(shard // 2) * 4 + block] & (1 << q)
                part = s_out[q * CB : (q + 1) * CB, start : start + D]
                score = bias[q * CB : (q + 1) * CB, :] - 0.5 * part
                pieces.append(jnp.where(allowed > 0, score, -jnp.inf))
            masked = jnp.concatenate(pieces, axis=0)
            s_out[:, start : start + D] = masked
            highest = jnp.max(masked, axis=0, keepdims=True)
            ms_out[0:1, start : start + D] = highest
            ms_out[1:2, start : start + D] = jnp.sum(jnp.exp(masked - highest), axis=0, keepdims=True)


def scores_of(scalars, shards, at, means, log_weights):
    per = 8
    whole = lambda shape: pl.BlockSpec(shape, lambda i, *f: (0,) * len(shape))
    return pl.pallas_call(
        score_kernel,
        out_shape=(
            jax.ShapeDtypeStruct((KC, NF), jnp.float32),
            jax.ShapeDtypeStruct((2, NF), jnp.float32),
            jax.ShapeDtypeStruct((D, NF), jnp.bfloat16),
        ),
        grid_spec=pltpu.PrefetchScalarGridSpec(
            num_scalar_prefetch=5,
            grid=(KC // per,),
            in_specs=[whole((SH, D))] * 4
            + [pl.BlockSpec((per, D, D), lambda i, *f: (i, 0, 0)), whole((KC, D)), whole((1, KC))],
            out_specs=[whole((KC, NF)), whole((2, NF)), whole((D, NF))],
            scratch_shapes=[pltpu.VMEM((KC, D), jnp.float32)],
        ),
        cost_estimate=pl.CostEstimate(
            flops=2 * KC * D * D * NF, bytes_accessed=4 << 20, transcendentals=KC * NF
        ),
        compiler_params=LIMIT,
        name="scores",
    )(*scalars, *shards, at, means, log_weights)


def log_total(parts, shard):
    rows = []
    for d, ref in enumerate(parts):
        start = (shard ^ d) * SH
        rows.append((ref[0:1, start : start + SH], ref[1:2, start : start + SH]))
    highest = functools.reduce(jnp.maximum, [m for m, _ in rows])
    total = sum(s * jnp.exp(m - highest) for m, s in rows)
    return highest + jnp.log(total)


def split_pair(value):
    high = value.astype(jnp.bfloat16).astype(jnp.float32)
    return high, value - high


def moment_kernel(own, meta, x0, x1, x2, x3, xt, scores, m0, m1, m2, m3, *refs):
    outs, (weights, left) = refs[:-2], refs[-2:]
    packed = outs[0]
    parts = (m0, m1, m2, m3)
    xs = (x0, x1, x2, x3)
    first = jnp.zeros((CB, D), jnp.float32)
    occupancy = jnp.zeros((CB, 1), jnp.float32)
    for shard in range(4):
        span = slice(shard * SH, (shard + 1) * SH)
        loglik = log_total(parts, shard)
        if own and shard == 0:
            outs[1][...] = loglik
        part = jnp.exp(scores[:, span] - loglik).astype(jnp.bfloat16)
        wide = part.astype(jnp.float32)
        weights[:, span] = wide
        occupancy += jnp.sum(wide, axis=1, keepdims=True)
        first += jnp.dot(part, xs[shard][...], preferred_element_type=jnp.float32)
    left_rows = left.shape[1]
    per = left_rows // D
    first_ref, occupancy_ref = outs[-2], outs[-1]
    first_ref[...] = first
    occupancy_ref[...] = jnp.broadcast_to(occupancy, (CB, D))
    row = lax.broadcasted_iota(jnp.int32, (D, D), 0)
    col = lax.broadcasted_iota(jnp.int32, (D, D), 1)
    row_half = lax.broadcasted_iota(jnp.int32, (HALF, D), 0)
    col_half = lax.broadcasted_iota(jnp.int32, (HALF, D), 1)
    keep_top = (col_half >= HALF) | (col_half >= row_half)
    for group in range(CB // per):
        places = [meta[1] ^ (group * per + c) for c in range(per)]
        buffer = left.at[group % left.shape[0]]
        for c in range(per):
            line = weights[pl.ds(places[c], 1), :].astype(jnp.bfloat16)
            buffer[c * D : (c + 1) * D, :] = xt[...] * line
        gram = None
        for shard in range(4):
            part = buffer[:, shard * SH : (shard + 1) * SH]
            term = jnp.dot(part, xs[shard][...], preferred_element_type=jnp.float32)
            gram = term if gram is None else gram + term
        for c in range(per):
            p = group * per + c
            one = gram[c * D : (c + 1) * D, :]
            diagonal = jnp.sum(jnp.where(row == col, one, 0.0), axis=0, keepdims=True)
            moved = pltpu.roll(one[HALF:, :], HALF, 1)
            triangle = jnp.where(keep_top, one[:HALF, :], moved)
            extras = [
                occupancy_ref[pl.ds(places[c], 1), :],
                first_ref[pl.ds(places[c], 1), :],
                diagonal,
            ]
            zero = jnp.zeros((1, D), jnp.float32)
            if own:
                tail = extras + [zero] * 5
            else:
                pairs = [split_pair(v) for v in extras]
                tail = [h for h, _ in pairs] + [l for _, l in pairs] + [zero] * 2
            packed[p, 0:HALF, :] = triangle.astype(packed.dtype)
            packed[p, HALF:ROWS, :] = jnp.concatenate(tail, axis=0).astype(packed.dtype)


def moments_of(chunk, meta, shards, xt, scores, partials):
    own = chunk == 0
    whole = lambda shape: pl.BlockSpec(shape, lambda i, f: (0,) * len(shape))
    out_shape = [jax.ShapeDtypeStruct((CB, ROWS, D), jnp.float32 if own else jnp.bfloat16)]
    out_specs = [whole((CB, ROWS, D))]
    if own:
        out_shape.append(jax.ShapeDtypeStruct((1, SH), jnp.float32))
        out_specs.append(whole((1, SH)))
    result = pl.pallas_call(
        functools.partial(moment_kernel, own),
        out_shape=tuple(out_shape),
        grid_spec=pltpu.PrefetchScalarGridSpec(
            num_scalar_prefetch=1,
            grid=(1,),
            in_specs=[whole((SH, D))] * 4
            + [whole((D, NF)), pl.BlockSpec((CB, NF), lambda i, f: (f[0] ^ chunk, 0))]
            + [whole((2, NF))] * 4,
            out_specs=out_specs,
            scratch_shapes=[
                pltpu.VMEM((CB, D), jnp.float32),
                pltpu.VMEM((CB, D), jnp.float32),
                pltpu.VMEM((CB, NF), jnp.float32),
                pltpu.VMEM((2, PER * D, NF), jnp.bfloat16),
            ],
        ),
        cost_estimate=pl.CostEstimate(
            flops=2 * CB * D * D * NF, bytes_accessed=2 << 20, transcendentals=CB * NF
        ),
        compiler_params=LIMIT,
        name="moments_own" if own else "moments",
    )(meta, *shards, xt, scores, *partials)
    return result if own else result[0]


def unpack_kernel(chunk, meta, packed, *refs):
    second, first, occupancy = refs[-3:]
    group = pl.program_id(0)
    lane = lax.broadcasted_iota(jnp.int32, (1, D), 1)

    @pl.when(group == 0)
    def _():
        occupancy[...] = refs[2][...] if chunk else jnp.zeros((1, D), jnp.float32)

    occupied = occupancy[...]
    row = lax.broadcasted_iota(jnp.int32, (D, D), 0)
    col = lax.broadcasted_iota(jnp.int32, (D, D), 1)
    unit = (row == col).astype(jnp.bfloat16)
    row_half = lax.broadcasted_iota(jnp.int32, (HALF, D), 0)
    col_half = lax.broadcasted_iota(jnp.int32, (HALF, D), 1)
    upper = (col_half >= HALF) | (col_half >= row_half)
    lower = (col_half < HALF) | (col_half - HALF < row_half)
    for c in range(8):
        p = meta[1] ^ (group * 8 + c)
        tile = packed[p, 0:HALF, :]
        extra = packed[p, HALF:ROWS, :].astype(jnp.float32)
        here = (meta[0] ^ chunk) * CB + group * 8 + c
        occupied = jnp.where(lane == here, extra[0:1, :] + extra[3:4, :], occupied)
        first[c : c + 1, :] = extra[1:2, :] + extra[4:5, :]
        diagonal = extra[2:3, :] + extra[5:6, :]
        largest = jnp.max(diagonal, axis=1, keepdims=True) * (1.0 / SPAN)
        turned = lax.dot_general(
            unit, tile, (((1,), (1,)), ((), ())), preferred_element_type=jnp.float32
        )
        wide = tile.astype(jnp.float32)
        both = jnp.concatenate([turned[:HALF, :], wide[:, :HALF]], axis=1)
        top = jnp.where(upper, wide, both)
        other = jnp.concatenate([turned[HALF:, :], wide[:, :HALF]], axis=1)
        mirror = jnp.concatenate([turned[HALF:, :], turned[:HALF, :]], axis=1)
        bottom = jnp.where(lower, other, mirror)
        full = jnp.concatenate([top, bottom], axis=0)
        size = (jnp.log2(jnp.abs(full)) + SPAN / 2) * largest
        entry = jnp.where(full < 0, -size, size)
        second[:, c, :] = jnp.where(row == col, diagonal, entry)
    occupancy[...] = occupied


def unpack(chunk, meta, packed, earlier):
    whole = lambda shape: pl.BlockSpec(shape, lambda i, f: (0,) * len(shape))
    place = lambda i, f: (f[0] ^ chunk) * 2 + i
    return pl.pallas_call(
        functools.partial(unpack_kernel, chunk),
        out_shape=(
            jax.ShapeDtypeStruct((D, KC, D), jnp.float32),
            jax.ShapeDtypeStruct((KC, D), jnp.float32),
            jax.ShapeDtypeStruct((1, D), jnp.float32),
        ),
        grid_spec=pltpu.PrefetchScalarGridSpec(
            num_scalar_prefetch=1,
            grid=(2,),
            in_specs=[whole((CB, ROWS, D))]
            + [pl.BlockSpec(memory_space=pl.ANY)] * len(earlier[:2])
            + [whole((1, D))] * len(earlier[2:]),
            out_specs=[
                pl.BlockSpec((D, 8, D), lambda i, f: (0, place(i, f), 0)),
                pl.BlockSpec((8, D), lambda i, f: (place(i, f), 0)),
                whole((1, D)),
            ],
        ),
        input_output_aliases={2 + n: n for n in range(len(earlier[:2]))},
        cost_estimate=pl.CostEstimate(
            flops=2 * CB * D * D * HALF, bytes_accessed=2 << 20, transcendentals=0
        ),
        compiler_params=LIMIT,
        name="unpack",
    )(meta, packed, *earlier)


def packed_pairs(total):
    extras = total[:, HALF : HALF + 3] + total[:, HALF + 3 : HALF + 6]
    high = lax.reduce_precision(extras, 8, 7)
    rest = (extras - high).astype(jnp.bfloat16)
    high = high.astype(jnp.bfloat16)
    spare = jnp.zeros((total.shape[0], 2, D), jnp.bfloat16)
    entries = total[:, :HALF].astype(jnp.bfloat16)
    return jnp.concatenate([entries, high, rest, spare], axis=1)


def decode(tile):
    wide = tile.astype(jnp.float32)
    largest = jnp.max(wide[HALF + 2 : HALF + 3] + wide[HALF + 5 : HALF + 6], axis=1, keepdims=True)
    codes = wide[:HALF]
    size = (jnp.log2(jnp.abs(codes)) + SPAN / 2) * (largest * (1.0 / SPAN))
    return jnp.where(codes < 0, -size, size), wide[HALF:]


def encode(out, c, entries, tail):
    extras = tail[0:3] + tail[3:6]
    high, rest = split_pair(extras)
    largest = jnp.max(extras[2:3], axis=1, keepdims=True)
    scale = 1.0 / jnp.maximum(largest, 1e-30)
    code = jnp.exp2(SPAN * jnp.minimum(jnp.abs(entries) * scale, 1.02) - SPAN / 2)
    out[c, 0:HALF, :] = jnp.where(entries < 0, -code, code).astype(jnp.bfloat16)
    rows = [high, rest, jnp.zeros((2, D), jnp.float32)]
    out[c, HALF:ROWS, :] = jnp.concatenate(rows, axis=0).astype(jnp.bfloat16)


def first_code_kernel(own, arrived, out):
    for c in range(out.shape[0]):
        total = own[c] + arrived[c].astype(jnp.float32)
        encode(out, c, total[:HALF], total[HALF:])


def next_code_kernel(mine, theirs, out):
    for c in range(out.shape[0]):
        one, one_tail = decode(mine[c])
        two, two_tail = decode(theirs[c])
        encode(out, c, one + two, one_tail + two_tail)


def code_sum(kernel, mine, theirs):
    size = theirs.size
    whole = pl.BlockSpec(theirs.shape, lambda i: (0, 0, 0))
    return pl.pallas_call(
        kernel,
        out_shape=jax.ShapeDtypeStruct(theirs.shape, jnp.bfloat16),
        grid=(1,),
        in_specs=[whole, whole],
        out_specs=whole,
        compiler_params=LIMIT,
        cost_estimate=pl.CostEstimate(
            flops=8 * size, bytes_accessed=8 * size, transcendentals=3 * size
        ),
        name=kernel.__name__,
    )(mine, theirs)


def per_device(frames, factors, comp_means, log_weights, pair_lists, counts):
    own = frames.reshape(SH, D)
    shards = (own, swap(own, "group", 1), swap(own, "loop", 1), swap_both(own))

    loop_index = lax.axis_index("loop")
    z_index = lax.axis_index("z")
    top = z_index >> 2
    low = (((z_index & 1) ^ top) * 8) + ((((z_index >> 1) & 1) ^ top) * 4)

    lists = (pair_lists, swap(pair_lists, "loop", 1))
    sizes = (counts, swap(counts, "loop", 1))
    meta = jnp.stack([lax.axis_index("y"), low]).astype(jnp.int32)

    at = jnp.transpose(factors, (1, 2, 0))
    scores, partial, xt = scores_of(
        (loop_index[None], *lists, *sizes), shards, at, comp_means, log_weights[None, :]
    )
    partials = (partial, swap(partial, "group", 1), swap(partial, "loop", 1), swap_both(partial))

    arrived = []
    for chunk in (2, 1, 3):
        packed = moments_of(chunk, meta, shards, xt, scores, partials)
        arrived.append(swap(packed, "y", chunk))
    total, loglik = moments_of(0, meta, shards, xt, scores, partials)
    for piece in arrived:
        total = total + piece.astype(jnp.float32)

    total = total[:8] + swap(packed_pairs(total[8:]), "z", Z_STEPS[0])
    arrived = swap(packed_pairs(total[4:]), "z", Z_STEPS[1])
    held = code_sum(first_code_kernel, total, arrived)
    held = code_sum(next_code_kernel, held, swap(held, "z", Z_STEPS[2]))
    held = code_sum(next_code_kernel, held, swap(held, "xh", 1))
    for step in reversed(Z_STEPS[:2]):
        held = jnp.concatenate([held, swap(held, "z", step)], axis=0)

    pieces = [held] + [swap(held, "y", chunk) for chunk in (1, 2, 3)]
    outs = ()
    for chunk, piece in enumerate(pieces):
        outs = unpack(chunk, meta, piece, outs)
    second, first, occupancy = outs
    return occupancy[0, :KC], first, second, loglik.reshape(4, D)


def solution(mesh):
    rep = mesh.shape["rep"]
    fine = Mesh(
        mesh.devices.reshape(2, 2, rep // 8, 4, 2), ("loop", "group", "z", "y", "xh")
    )
    reps = ("z", "y", "xh")
    return jax.shard_map(
        per_device,
        mesh=fine,
        in_specs=(
            P(("loop",) + reps, "group", None),
            P(None, ("loop", "group"), None),
            P(("loop", "group"), None),
            P(("loop", "group")),
            P(("loop",) + reps, "group", None, None),
            P(("loop",) + reps, "group", None),
        ),
        out_specs=(
            P(("loop", "group")),
            P(("loop", "group"), None),
            P(None, ("loop", "group"), None),
            P(("loop",) + reps, "group"),
        ),
        check_vma=False,
    )
```
